32 devices in a mesh: section: 4 (over y, core), space: 8 (over z, x).
Axes of the slice: x: 2, y: 2, z: 4, core: 2. Of those that a mesh axis runs over, the one named last changes fastest.
Arguments:
- features: bfloat16 [4, 2048, 256], P('section', 'space'), may hold values from -6 to 6
- out_grad: bfloat16 [4, 2048, 256], P('section', 'space'), may hold values from -6 to 6
- weight: bfloat16 [4, 27, 256, 256], P('section'), may hold values from -0.078125 to 0.078125
- counts: int32 [4, 16], P('section', 'space'), may hold values from 16 to 128
- local_rows: int32 [4, 27, 2048], P('section', None, 'space'), may hold values from -1 to 255, as said below
- send_rows: int32 [4, 8, 27, 8, 2], P('section', 'space'), may hold values from -1 to 255, as said below
- recv_rows: int32 [4, 8, 27, 8, 2], P('section', 'space'), may hold values from -1 to 255, as said below
Outputs:
- handoff: bfloat16 [4, 2048, 256], P('section', 'space')
- weight_grad: float32 [4, 6912, 256], P('section', 'space')
The draws below stay inside these ranges and needn't reach their ends.
Inputs may be any that keep to these rules, and one draw needn't show every extreme that they name: `local_rows`: -1 where a voxel has no pair on its own device at that offset. `send_rows`: for each offset and two different devices, the first 1 to 2 slots are used and the rest are -1; a device's slots to itself are all -1; for every sending device there is one offset at which all 2 slots to every other device are used. `recv_rows`: slot for slot the pairs of send_rows seen from the receiving device, -1 in the same empty slots.
All inputs are finite; a program needn't handle non-finite values.
Results may differ from the reference program's by a relative error of at most 0.0019.
Values may be sent and summed in bfloat16 or wider, within the bound.
No kernel may reach another device: no remote copies, remote signals or barrier semaphores. Data moves between devices by JAX's collectives and lax.ppermute only.
A program may use at most 64 MiB of HBM per device.

```python
import jax
import jax.numpy as jnp
from jax import lax

C = 256
K = 27
BLOCK = 128
VOX_DEV = 256
VOX = 2048
NBLK = 16
CAP = 2
N_SECTION = 4
N_SPACE = 8


def draw_local_rows(key, part):
    first, second = jax.random.split(jax.random.fold_in(key, 3))
    shape = (N_SECTION, K, VOX)
    rows_drawn = jax.random.randint(first, shape, 0, VOX_DEV)
    dropped = jax.random.randint(second, shape, 0, 4) == 0
    return jnp.where(dropped, -1, rows_drawn).astype(jnp.int32)


def route_tables(key):
    base = jax.random.fold_in(key, 17)
    key_count, key_full, key_target, key_source = jax.random.split(base, 4)
    shape = (N_SECTION, N_SPACE, K, N_SPACE)
    used = jax.random.randint(key_count, shape, 1, CAP + 1)
    full_at = jax.random.randint(key_full, (N_SECTION, N_SPACE, 1, 1), 0, K)
    used = jnp.where(jnp.arange(K)[None, None, :, None] == full_at, CAP, used)
    same = jnp.arange(N_SPACE)[:, None] == jnp.arange(N_SPACE)[None, :]
    used = jnp.where(same[None, :, None, :], 0, used)
    live = jnp.arange(CAP)[None, None, None, None, :] < used[..., None]
    target_rows = jax.random.randint(key_target, shape + (CAP,), 0, VOX_DEV)
    source_rows = jax.random.randint(key_source, shape + (CAP,), 0, VOX_DEV)
    return (jnp.where(live, target_rows, -1).astype(jnp.int32), jnp.where(live, source_rows, -1).astype(jnp.int32))


def draw_send_rows(key, part):
    return route_tables(key)[0]


def draw_recv_rows(key, part):
    return jnp.transpose(route_tables(key)[1], (0, 3, 2, 1, 4))


def with_ends(drawn, key, smallest, top_value):
    longest = drawn.shape.index(max(drawn.shape))
    spots = []
    for shift in (0, 1):
        where = [jax.random.randint(jax.random.fold_in(key, axis), (), 0, length) for axis, length in enumerate(drawn.shape)]
        where[longest] = (where[longest] + shift) % drawn.shape[longest]
        spots.append(tuple(where))
    return drawn.at[spots[0]].set(smallest).at[spots[1]].set(top_value)


def block_levels(rng, extent, pieces, low, high):
    loudness = 1.0
    for position, blocks in pieces:
        steps = jax.random.uniform(jax.random.fold_in(jax.random.fold_in(rng, 6), position), (blocks,), jnp.float32, low / len(pieces), high / len(pieces))
        loudness = loudness * jnp.repeat(jnp.exp(steps), extent[position] // blocks).reshape((-1,) + (1,) * (len(extent) - 1 - position))
    return loudness


def normal_values(rng, shape, scale, limit, shards=(), held_as=jnp.bfloat16):
    gain = block_levels(rng, shape, shards, -0.22, 0.18) if shards else 1.0
    array = jax.random.normal(rng, shape, jnp.float32) * scale * gain
    return jnp.minimum(jnp.maximum(array, -limit), limit).astype(held_as)


def setup_inputs(seed: int = 0) -> dict:
    splits = jax.random.split(jax.random.key(seed), 8)
    features = normal_values(splits[0], (N_SECTION, VOX, C), 1.0, 6.0, ((0, 4), (1, 8)))
    out_grad = normal_values(splits[1], (N_SECTION, VOX, C), 1.0, 6.0, ((0, 4), (1, 8)))
    weight = normal_values(splits[2], (N_SECTION, K, C, C), (K * C) ** -0.5, 0.078125, ((0, 4),))
    counts = with_ends(jax.random.randint(splits[3], (N_SECTION, NBLK), 16, BLOCK + 1), jax.random.fold_in(splits[3], 1), 16, BLOCK).astype(jnp.int32)
    local_rows = draw_local_rows(jax.random.fold_in(splits[7], 71), 0)
    send_rows = draw_send_rows(jax.random.fold_in(splits[7], 71), 0)
    recv_rows = draw_recv_rows(jax.random.fold_in(splits[7], 71), 0)
    return {"features": features, "out_grad": out_grad, "weight": weight, "counts": counts, "local_rows": local_rows, "send_rows": send_rows, "recv_rows": recv_rows}


def one_section(packed):
    inputs_all, grads_all, kernel, block_counts, local_map, send_map, recv_map = packed
    inside = (jnp.arange(BLOCK, dtype=jnp.int32)[None, :] < block_counts[:, None]).reshape(N_SPACE, VOX_DEV, 1)
    nothing = jnp.zeros((), inputs_all.dtype)
    xmask = jnp.where(inside, inputs_all.reshape(N_SPACE, VOX_DEV, C), nothing)
    gmask = jnp.where(inside, grads_all.reshape(N_SPACE, VOX_DEV, C), nothing)
    kernel_wide = kernel.astype(jnp.float32)
    local_all = local_map.reshape(K, N_SPACE, VOX_DEV)

    def local_step(carry, device):
        index_map = local_all[:, device, :].T
        rows_g = gmask[device]
        gathered = jnp.where((index_map >= 0)[:, :, None], rows_g[jnp.maximum(index_map, 0)], nothing).astype(jnp.float32)
        input_part = jnp.einsum('vko,koi->vi', gathered, kernel_wide)
        weight_part = jnp.einsum('vko,vi->koi', gathered, xmask[device].astype(jnp.float32))
        return carry + weight_part, input_part

    weight_sum, local_grads = lax.scan(local_step, jnp.zeros((K, C, C), jnp.float32), jnp.arange(N_SPACE, dtype=jnp.int32))
    flat_x = xmask.reshape(-1, C)

    def remote_step(carry, sender):
        grads_acc, weights_acc = carry
        sent = send_map[sender]
        got = jnp.transpose(recv_map[:, :, sender, :], (1, 0, 2))
        grad_rows = jnp.where((sent >= 0)[..., None], gmask[sender][jnp.maximum(sent, 0)], nothing).astype(jnp.float32)
        partial_value = jnp.einsum('kpso,koi->kpsi', grad_rows, kernel_wide)
        partial_value = lax.optimization_barrier(partial_value.astype(jnp.bfloat16)).astype(jnp.float32)
        owners = jnp.arange(N_SPACE, dtype=jnp.int32)[None, :, None]
        target = jnp.where(got >= 0, owners * VOX_DEV + got, N_SPACE * VOX_DEV).reshape(-1).astype(jnp.int32)
        grads_acc = grads_acc.at[target].add(partial_value.reshape(-1, C), mode="drop")
        picked = flat_x[jnp.minimum(target, N_SPACE * VOX_DEV - 1)].reshape(got.shape + (C,))
        source_rows = jnp.where((got >= 0)[..., None], picked, nothing).astype(jnp.float32)
        weights_acc = weights_acc + jnp.einsum('kpso,kpsi->koi', grad_rows, source_rows)
        return (grads_acc, weights_acc), None

    (input_all, weight_sum), _ = lax.scan(remote_step, (local_grads.reshape(-1, C), weight_sum), jnp.arange(N_SPACE, dtype=jnp.int32))
    result = jnp.where(inside.reshape(-1, 1), input_all, 0.0).astype(jnp.bfloat16)
    return result, (weight_sum * (VOX ** -0.5)).reshape(K * C, C)


def reference(features, out_grad, weight, counts, local_rows, send_rows, recv_rows):
    results, weight_grad = lax.map(one_section, (features, out_grad, weight, counts, local_rows, send_rows, recv_rows))
    handoff = jnp.concatenate([results[1:], jnp.zeros_like(results[:1])], axis=0)
    return (handoff, weight_grad)
```

```python
import functools
import math

import jax
import jax.numpy as jnp
from jax import lax
from jax.experimental import pallas as pl
from jax.experimental.pallas import tpu as pltpu
from jax.sharding import PartitionSpec as P

BLOCK = 128
LANES = 128
F32 = jnp.float32
BF16 = jnp.bfloat16


def ring_order(mesh):
    n = mesh.shape["space"]
    try:
        axis = mesh.axis_names.index("space")
        line = mesh.devices.swapaxes(0, axis).reshape(n, -1)[:, 0]
        place = {(d.coords[2], d.coords[0]): i for i, d in enumerate(line)}
    except Exception:
        return list(range(n))
    zs = sorted({z for z, _ in place})
    xs = sorted({x for _, x in place})
    if len(place) != n or len(zs) * len(xs) != n or len(xs) < 2 or len(zs) % 2:
        return list(range(n))
    walk = []
    for turn, z in enumerate(zs):
        inner = xs[1:] if turn % 2 == 0 else xs[:0:-1]
        walk += [(z, x) for x in inner]
    walk += [(z, xs[0]) for z in reversed(zs)]
    return [place[p] for p in walk]


def iota(shape, axis):
    return lax.broadcasted_iota(jnp.int32, shape, axis).astype(F32)


def valid_rows(counts_ref, shape):
    row = lax.broadcasted_iota(jnp.int32, shape, 0)
    inside = row < counts_ref[0, 0]
    for b in range(1, shape[0] // BLOCK):
        inside = inside | ((row >= b * BLOCK) & (row < b * BLOCK + counts_ref[0, b]))
    return inside


def pick(table, index):
    out = jnp.int32(table[0])
    for i in range(1, len(table)):
        out = jnp.where(index == i, jnp.int32(table[i]), out)
    return out


def dot(a, b, ca=1, cb=0):
    return lax.dot_general(a, b, (((ca,), (cb,)), ((), ())), preferred_element_type=F32)


class Plan:
    def __init__(self, mesh, rows, channels, offsets):
        self.n = n = mesh.shape["space"]
        self.ring = ring_order(mesh)
        self.rows, self.c, self.k = rows, channels, offsets
        self.out_rows = offsets * channels // n
        self.align = math.gcd(self.out_rows, channels)
        self.span = max(
            -(-(d * self.out_rows % channels + self.out_rows) // channels) for d in range(n)
        )
        self.kpad = -(-(offsets + self.span) // 16) * 16
        self.pairs = 2 * n
        self.at_x = channels
        self.at_l = channels + rows
        self.at_t = self.at_l + self.kpad
        self.block_rows = self.at_t + self.pairs
        self.scale = float(rows * n) ** (-0.5)

    def owner(self, me, step):
        where = {d: i for i, d in enumerate(self.ring)}
        return pick([self.ring[(where[d] - step) % self.n] for d in range(self.n)], me)

    def first_offset(self, me):
        return (me * self.out_rows) // self.c


def pack_kernel(plan, counts_ref, x_ref, g_ref, l_ref, s_ref, r_ref, out_ref, lscr, tscr):
    inside = valid_rows(counts_ref, (plan.rows, plan.c))
    x = jnp.where(inside, x_ref[0].astype(F32), 0.0)
    g = jnp.where(inside, g_ref[0].astype(F32), 0.0)
    out_ref[: plan.c] = jnp.transpose(g).astype(BF16)
    out_ref[plan.at_x : plan.at_l] = x.astype(BF16)
    lscr[...] = jnp.full(lscr.shape, -1, jnp.int32)
    for k in range(plan.k):
        lscr[k : k + 1] = l_ref[k]
    out_ref[plan.at_l : plan.at_t] = lscr[...].astype(F32).astype(BF16)
    tscr[...] = jnp.full(tscr.shape, -1, jnp.int32)
    for p in range(plan.n):
        tscr[2 * p : 2 * p + 2, : plan.k] = s_ref[p]
        tscr[2 * p : 2 * p + 2, LANES : LANES + plan.k] = r_ref[p]
    out_ref[plan.at_t :] = tscr[...].astype(F32).astype(BF16)


def local_kernel(plan, block_ref, w_ref, out_ref, scat_ref, lscr):
    g = jnp.transpose(block_ref[: plan.c].astype(F32)).astype(BF16)
    lscr[...] = jnp.zeros(lscr.shape, F32)
    lscr[: plan.kpad] = block_ref[plan.at_l : plan.at_t].astype(F32)
    columns = jnp.transpose(lscr[...])
    lane = iota((plan.rows, plan.rows), 1)
    acc = jnp.zeros((plan.rows, plan.c), F32)
    for k in range(plan.k):
        hot = (columns[:, k : k + 1] == lane).astype(F32).astype(BF16)
        rows = dot(hot, g).astype(BF16)
        acc = acc + dot(rows, w_ref[0, k])
    out_ref[...] = acc
    table = block_ref[plan.at_t :, LANES:].astype(F32)
    lane = iota((plan.pairs, plan.rows), 1)
    for k in range(plan.k):
        hot = (table[:, k : k + 1] == lane).astype(F32)
        scat_ref[k * plan.pairs : (k + 1) * plan.pairs] = hot.astype(BF16)


def remote_rows(plan, block_ref, me, owner, r_ref):
    table = block_ref[plan.at_t :, :LANES].astype(F32)
    turned = jnp.transpose(table)[: plan.kpad]
    lane = lax.broadcasted_iota(jnp.int32, turned.shape, 1)
    wide = iota((plan.kpad, plan.rows), 1)
    hots = []
    for q in range(2):
        column = jnp.sum(jnp.where(lane == 2 * me + q, turned, 0.0), axis=1, keepdims=True)
        hots.append((column == wide).astype(F32))
    hot = jnp.concatenate(hots, axis=0).astype(BF16)
    rows = dot(hot, block_ref[: plan.c], 1, 1)
    size = 2 * plan.kpad
    where = pl.ds(pl.multiple_of(owner * size, size), size)
    for h in range(plan.c // LANES):
        r_ref[h, where] = rows[:, h * LANES : (h + 1) * LANES]


def weight_part(plan, block_ref, me, owner, acc_ref, a_ref, b_ref, lscr, first):
    gt = block_ref[: plan.c]
    x = block_ref[plan.at_x : plan.at_l]
    lscr[...] = block_ref[plan.at_l : plan.at_t].astype(F32)
    table = block_ref[plan.at_t :].astype(F32)
    k0 = plan.first_offset(me)
    tall = iota((plan.rows, plan.rows), 0)
    lane = lax.broadcasted_iota(jnp.int32, (plan.pairs, LANES), 1)
    wide = iota((plan.pairs, plan.rows), 1)
    hots_g, hots_x = [], []
    for kk in range(plan.span):
        row = lscr[pl.ds(k0 + kk, 1)]
        hot = (row == tall).astype(F32).astype(BF16)
        picked = dot(gt, hot).astype(BF16)
        term = dot(picked, x)
        rows = pl.ds(kk * plan.c, plan.c)
        acc_ref[rows] = term if first else acc_ref[rows] + term
        here = lane == k0 + kk
        for side, hots in ((0, hots_g), (1, hots_x)):
            values = table[:, side * LANES : (side + 1) * LANES]
            column = jnp.sum(jnp.where(here, values, 0.0), axis=1, keepdims=True)
            hots.append((column == wide).astype(F32))
    rows_g = dot(jnp.concatenate(hots_g, axis=0).astype(BF16), gt, 1, 1).astype(BF16)
    rows_x = dot(jnp.concatenate(hots_x, axis=0).astype(BF16), x).astype(BF16)
    for kk in range(plan.span):
        start = kk * plan.n * plan.pairs + owner * plan.pairs
        rows = pl.ds(pl.multiple_of(start, plan.pairs), plan.pairs)
        part = slice(kk * plan.pairs, (kk + 1) * plan.pairs)
        a_ref[rows] = rows_g[part]
        b_ref[rows] = rows_x[part]


def arrive_kernel(plan, steps, first, *refs):
    blocks = refs[: len(steps)]
    acc_ref, a_ref, b_ref, r_ref, lscr = refs[-5:]
    me = lax.axis_index("space")
    if not first:
        for new, old in zip((acc_ref, a_ref, b_ref, r_ref), refs[len(steps) :]):
            new[...] = old[...]
    for i, (step, block_ref) in enumerate(zip(steps, blocks)):
        owner = plan.owner(me, step)
        remote_rows(plan, block_ref, me, owner, r_ref)
        weight_part(plan, block_ref, me, owner, acc_ref, a_ref, b_ref, lscr, first and i == 0)


def grad_kernel(plan, steps, *refs):
    blocks = refs[: len(steps)]
    counts_ref, local_ref, scat_ref, w_ref, r_in, out_ref, r_ref, part_ref = refs[len(steps) :]
    me = lax.axis_index("space")
    r_ref[...] = r_in[...]
    for step, block_ref in zip(steps, blocks):
        remote_rows(plan, block_ref, me, plan.owner(me, step), r_ref)
    for k in range(plan.k):
        halves = [
            r_ref[h, pl.ds(k, plan.pairs, stride=plan.kpad)] for h in range(plan.c // LANES)
        ]
        rows = jnp.concatenate(halves, axis=1).astype(BF16)
        part_ref[k * plan.pairs : (k + 1) * plan.pairs] = dot(rows, w_ref[0, k]).astype(BF16)
    grad = local_ref[...] + dot(scat_ref[...], part_ref[...], 0, 0)
    inside = valid_rows(counts_ref, (plan.rows, plan.c))
    out_ref[...] = jnp.where(inside, grad, 0.0).astype(BF16)


def last_kernel(plan, steps, *refs):
    blocks = refs[: len(steps)]
    acc_in, a_in, b_in, out_ref, acc_ref, a_ref, b_ref, lscr = refs[len(steps) :]
    me = lax.axis_index("space")
    acc_ref[...] = acc_in[...]
    a_ref[...] = a_in[...]
    b_ref[...] = b_in[...]
    for step, block_ref in zip(steps, blocks):
        weight_part(plan, block_ref, me, plan.owner(me, step), acc_ref, a_ref, b_ref, lscr, False)
    size = plan.n * plan.pairs
    left = lax.broadcasted_iota(jnp.int32, (size, size), 0)
    right = lax.broadcasted_iota(jnp.int32, (size, size), 1)
    turned = (left % plan.pairs // 2) * plan.pairs + (left // plan.pairs) * 2 + left % 2
    swap = (turned == right).astype(F32).astype(BF16)
    for kk in range(plan.span):
        rows = pl.ds(kk * size, size)
        rows_x = dot(swap, b_ref[rows]).astype(BF16)
        acc_ref[pl.ds(kk * plan.c, plan.c)] += dot(a_ref[rows], rows_x, 0, 0)
    start = me * plan.out_rows - plan.first_offset(me) * plan.c
    rows = pl.ds(pl.multiple_of(start, plan.align), plan.out_rows)
    out_ref[0] = acc_ref[rows] * plan.scale


def vmem(count):
    return [pl.BlockSpec(memory_space=pltpu.VMEM)] * count


def body(mesh, features, out_grad, weight, counts, local_rows, send_rows, recv_rows):
    rows, channels = features.shape[1:]
    offsets = weight.shape[1]
    plan = Plan(mesh, rows, channels, offsets)
    n = plan.n
    smem = [pl.BlockSpec(memory_space=pltpu.SMEM)]
    turned_l = jnp.transpose(local_rows, (1, 0, 2))
    turned_s = jnp.transpose(send_rows[0, 0], (1, 2, 0))
    turned_r = jnp.transpose(recv_rows[0, 0], (1, 2, 0))
    block = pl.pallas_call(
        functools.partial(pack_kernel, plan),
        out_shape=jax.ShapeDtypeStruct((plan.block_rows, channels), BF16),
        in_specs=smem + vmem(5),
        out_specs=vmem(1)[0],
        scratch_shapes=[
            pltpu.VMEM((plan.kpad, channels), jnp.int32),
            pltpu.VMEM((plan.pairs, channels), jnp.int32),
        ],
        name="pack",
    )(counts, features, out_grad, turned_l, turned_s, turned_r)

    ring = plan.ring
    forth = [(ring[i], ring[(i + 1) % n]) for i in range(n)]
    back = [(b, a) for a, b in forth]
    ups, downs = [block], [block]
    for _ in range(n // 2):
        ups.append(lax.ppermute(ups[-1], "space", forth))
        if len(ups) + len(downs) < n + 1:
            downs.append(lax.ppermute(downs[-1], "space", back))

    local, scat = pl.pallas_call(
        functools.partial(local_kernel, plan),
        out_shape=(
            jax.ShapeDtypeStruct((rows, channels), F32),
            jax.ShapeDtypeStruct((offsets * plan.pairs, rows), BF16),
        ),
        in_specs=vmem(2),
        out_specs=tuple(vmem(2)),
        scratch_shapes=[pltpu.VMEM((LANES, rows), F32)],
        cost_estimate=pl.CostEstimate(flops=4 * offsets * rows**3, bytes_accessed=2 * weight.size, transcendentals=0),
        name="local",
    )(block, weight)

    size = plan.n * plan.pairs
    state_shapes = (
        jax.ShapeDtypeStruct((plan.span * channels, channels), F32),
        jax.ShapeDtypeStruct((plan.span * size, channels), BF16),
        jax.ShapeDtypeStruct((plan.span * size, channels), BF16),
        jax.ShapeDtypeStruct((channels // LANES, plan.pairs * plan.kpad, LANES), F32),
    )
    state = ()
    rounds = [[0, 1, -1]] + [[s, -s] for s in range(2, len(downs))]
    last = [s for s in range(len(downs), len(ups))]
    for steps in rounds:
        blocks = [ups[s] if s >= 0 else downs[-s] for s in steps]
        m = len(blocks)
        state = pl.pallas_call(
            functools.partial(arrive_kernel, plan, steps, not state),
            out_shape=state_shapes,
            in_specs=vmem(m + len(state)),
            out_specs=tuple(vmem(4)),
            scratch_shapes=[pltpu.VMEM((plan.kpad, rows), F32)],
            cost_estimate=pl.CostEstimate(flops=6 * m * plan.span * rows**3, bytes_accessed=4 * 2**20, transcendentals=0),
            name="arrive",
        )(*blocks, *state)
    acc, a, b, r = state
    blocks = [ups[s] for s in last]
    result = pl.pallas_call(
        functools.partial(grad_kernel, plan, last),
        out_shape=jax.ShapeDtypeStruct((rows, channels), BF16),
        in_specs=vmem(len(last)) + smem + vmem(4),
        out_specs=vmem(1)[0],
        scratch_shapes=[
            pltpu.VMEM(state_shapes[3].shape, F32),
            pltpu.VMEM((offsets * plan.pairs, channels), BF16),
        ],
        cost_estimate=pl.CostEstimate(flops=4 * offsets * rows**3, bytes_accessed=4 * 2**20, transcendentals=0),
        name="grad",
    )(*blocks, counts, local, scat, weight, r)
    sections = lax.axis_size("section")
    handoff = lax.ppermute(result, "section", [(i + 1, i) for i in range(sections - 1)])
    weight_grad = pl.pallas_call(
        functools.partial(last_kernel, plan, last),
        out_shape=jax.ShapeDtypeStruct((1, plan.out_rows, channels), F32),
        in_specs=vmem(len(last) + 3),
        out_specs=vmem(1)[0],
        scratch_shapes=[
            pltpu.VMEM(state_shapes[0].shape, F32),
            pltpu.VMEM(state_shapes[1].shape, BF16),
            pltpu.VMEM(state_shapes[2].shape, BF16),
            pltpu.VMEM((plan.kpad, rows), F32),
        ],
        cost_estimate=pl.CostEstimate(flops=6 * plan.span * rows**3, bytes_accessed=4 * 2**20, transcendentals=0),
        name="last",
    )(*blocks, acc, a, b)
    return (handoff[None], weight_grad)


def solution(mesh):
    placed = (
        P("section", "space", None),
        P("section", "space", None),
        P("section", None, None, None),
        P("section", "space"),
        P("section", None, "space"),
        P("section", "space", None, None, None),
        P("section", "space", None, None, None),
    )
    return jax.shard_map(
        functools.partial(body, mesh),
        mesh=mesh,
        in_specs=placed,
        out_specs=(P("section", "space", None), P("section", "space", None)),
        check_vma=False,
    )
```
